128 devices in a mesh: expert: 128 (over x, z, y, core).
Axes of the slice: x: 4, y: 4, z: 4, core: 2. Of those that a mesh axis runs over, the one named last changes fastest.
Arguments:
- routed_rows: bfloat16 [24576, 2048], P('expert'), may hold values from -6 to 6
- expert_index: int32 [24576, 1], P('expert'), may hold values from 0 to 127; in each aligned block of 192 rows (0 to 191, 192 to 383, ...) at most 3 rows name the same one
- route_weight: float32 [24576], P('expert'), may hold values from 0.1 to 1
- cotangent: bfloat16 [24576, 2048], P('expert'), may hold values from -6 to 6
- gate_weight: bfloat16 [128, 2048, 768], P('expert'), may hold values from -0.125 to 0.125
- up_weight: bfloat16 [128, 2048, 768], P('expert'), may hold values from -0.125 to 0.125
- down_weight: bfloat16 [128, 768, 2048], P('expert'), may hold values from -0.21875 to 0.21875
Outputs:
- layer_out: bfloat16 [24576, 2048], P('expert')
- row_grad: bfloat16 [24576, 2048], P('expert')
- weight_grad: float32 [24576], P('expert')
- gate_grad: bfloat16 [128, 2048, 768], P('expert')
- up_grad: bfloat16 [128, 2048, 768], P('expert')
- down_grad: bfloat16 [128, 768, 2048], P('expert')
The draws below stay inside these ranges and needn't reach their ends.
Inputs may be any that keep to these rules, and one draw needn't show every extreme that they name: `expert_index`: among the 192 rows of one device no expert is named more than 3 times, a bound that some block reaches.
All inputs are finite; a program needn't handle non-finite values.
Results may differ from the reference program's by a relative error of at most 0.0058.
Values may be sent and summed in bfloat16 or wider, within the bound.
No kernel may reach another device: no remote copies, remote signals or barrier semaphores. Data moves between devices by JAX's collectives and lax.ppermute only.
A program may use at most 128 MiB of HBM per device.

```python
import math
import jax
import jax.numpy as jnp
import numpy as np
from jax import lax

D = 2048
FF = 768
ROW_DEV = 192
EXPERTS = 128
ROWS = 24576
CAP = 3
N_EXPERT = 128


def steps_of(rng, extent, pieces, low, largest):
    def one(dim, parts):
        draws = jax.random.uniform(jax.random.fold_in(jax.random.fold_in(rng, 6), dim), (parts,), jnp.float32, low / len(pieces), largest / len(pieces))
        return jnp.repeat(jnp.exp(draws), extent[dim] // parts).reshape((-1,) + (1,) * (len(extent) - dim - 1))

    gain = one(*pieces[0])
    for cut in pieces[1:]:
        gain = gain * one(*cut)
    return gain


def shared_out(own_key, own, number, rows, number_of, top, limit, skew):
    sequence = jax.random.permutation(own_key, number_of)
    heavy_load, ordinary = shares(number_of, rows * top, limit, skew, True), shares(number_of, rows * top, limit, skew, False)
    places = jnp.arange(number_of)

    def named(lengths, turn):
        used = int((lengths > 0).sum())
        fixed = max(1, used // 4)
        moved = fixed + (places - fixed + turn * (used - fixed)) % max(1, number_of - fixed)
        return jnp.zeros((number_of,), jnp.int32).at[sequence[jnp.where(places < fixed, places, moved)]].set(jnp.asarray(lengths, jnp.int32))

    lengths = jnp.where(number % 4 == 0, named(heavy_load, number // 4), named(ordinary, number - number // 4 - 1))
    mixed = jax.random.permutation(jax.random.fold_in(own, 3), number_of)
    donor, receiver = mixed[0:number_of // 2 * 2:2], mixed[1:number_of // 2 * 2:2]
    margin = jnp.minimum(lengths[donor] - 1, limit - lengths[receiver]) // 2
    margin = jnp.where((donor == sequence[0]) | (receiver == sequence[0]) | (lengths[receiver] == 0), 0, jnp.maximum(margin, 0))
    moved = jax.random.randint(jax.random.fold_in(own, 4), (number_of // 2,), 0, 1 << 20) % (margin + 1)
    lengths = lengths.at[donor].add(-moved).at[receiver].add(moved)
    labels = jnp.searchsorted(jnp.cumsum(lengths), jnp.arange(rows * top), side="right").astype(jnp.int32)
    grid = labels.reshape(top, rows).T
    grid = grid[jax.random.permutation(jax.random.fold_in(own, 1), rows)]
    turn = jax.random.randint(jax.random.fold_in(own, 2), (rows, 1), 0, top)
    return jnp.take_along_axis(grid, (jnp.arange(top)[None, :] + turn) % top, axis=1)


def shares(amount, total, limit, slope, full):
    weights = [(1 << 20) // math.isqrt(rank ** slope) + 1 for rank in range(1, amount + 1)]
    largest = limit if full else min(limit, max(-(-total // amount), total * weights[0] // sum(weights)))
    least = 1 if total - largest >= amount - 1 else 0
    given, rest = [largest] + [least] * (amount - 1), total - largest - least * (amount - 1)
    while rest > 0:
        free = [i for i in range(1, amount) if given[i] < largest] or [i for i in range(1, amount) if given[i] < limit]
        pool, budget = sum([weights[i] for i in free]), rest
        for i in free:
            more = min(limit - given[i], max(1, budget * weights[i] // pool), rest)
            given[i] = given[i] + more
            rest = rest - more
    return np.array(given)


def scatter_about(own_key, extent, width, most, shards=(), held_as=jnp.bfloat16):
    values = jax.random.normal(own_key, extent, jnp.float32) * width
    if len(shards) > 0:
        values = steps_of(own_key, extent, shards, -0.22, 0.18) * values
    return jnp.clip(values, min=-most, max=most).astype(held_as)


def setup_inputs(seed: int = 0) -> dict:
    arg_keys = jax.random.split(jax.random.key(seed), 8)
    routed_rows = scatter_about(arg_keys[0], (ROWS, D), 1.0, 6.0, ((0, 128),))
    expert_index_keys = jax.random.split(jax.random.fold_in(arg_keys[1], 1), ROWS // ROW_DEV)
    expert_index_turns = jax.random.permutation(jax.random.fold_in(arg_keys[1], 3), ROWS // ROW_DEV)
    expert_index = jax.vmap(lambda own, number: shared_out(jax.random.fold_in(arg_keys[1], 2), own, number, ROW_DEV, EXPERTS, 1, CAP, 2))(expert_index_keys, expert_index_turns).reshape((ROWS, 1))
    route_weight = jnp.clip(jnp.exp(math.log(1.0) - 2.3025851 * jax.random.uniform(arg_keys[2], (ROWS,), jnp.float32) ** steps_of(arg_keys[2], (ROWS,), ((0, 128),), -0.2, 0.2)), 0.1, 1.0)
    cotangent = scatter_about(arg_keys[3], (ROWS, D), 1.0, 6.0, ((0, 128),))
    gate_weight = scatter_about(arg_keys[4], (EXPERTS, D, FF), D ** -0.5, 0.125, ((0, 128),))
    up_weight = scatter_about(arg_keys[5], (EXPERTS, D, FF), D ** -0.5, 0.125, ((0, 128),))
    down_weight = scatter_about(arg_keys[6], (EXPERTS, FF, D), FF ** -0.5, 0.21875, ((0, 128),))
    return dict(routed_rows=routed_rows, expert_index=expert_index, route_weight=route_weight, cotangent=cotangent, gate_weight=gate_weight, up_weight=up_weight, down_weight=down_weight)


def expert_pass(inputs):
    rows_in, out_grad, w_gate, w_up, w_down = inputs
    gate_act = jnp.dot(rows_in, w_gate, preferred_element_type=jnp.float32)
    up_act = jnp.dot(rows_in, w_up, preferred_element_type=jnp.float32)
    sigma = jax.nn.sigmoid(gate_act)
    silu_gate = gate_act * sigma
    hidden = (silu_gate * up_act).astype(jnp.bfloat16)
    expert_out = jnp.dot(hidden, w_down, preferred_element_type=jnp.float32).astype(jnp.bfloat16)
    hidden_grad = jnp.dot(out_grad, w_down.T, preferred_element_type=jnp.float32)
    gate_pre = (hidden_grad * up_act * sigma * (1.0 + gate_act * (1.0 - sigma))).astype(jnp.bfloat16)
    up_pre = (hidden_grad * silu_gate).astype(jnp.bfloat16)
    input_grad = (jnp.dot(gate_pre, w_gate.T, preferred_element_type=jnp.float32)
                  + jnp.dot(up_pre, w_up.T, preferred_element_type=jnp.float32)).astype(jnp.bfloat16)
    gate_grad = jnp.dot(rows_in.T, gate_pre, preferred_element_type=jnp.float32).astype(jnp.bfloat16)
    up_grad = jnp.dot(rows_in.T, up_pre, preferred_element_type=jnp.float32).astype(jnp.bfloat16)
    down_grad = jnp.dot(hidden.T, out_grad, preferred_element_type=jnp.float32).astype(jnp.bfloat16)
    return expert_out, input_grad, gate_grad, up_grad, down_grad


def reference(routed_rows, expert_index, route_weight, cotangent, gate_weight, up_weight, down_weight):
    choice_ids = expert_index[:, 0]
    devices = N_EXPERT
    per_expert = devices * CAP
    onehot = (choice_ids[:, None] == jnp.arange(EXPERTS, dtype=jnp.int32)[None, :]).astype(jnp.int32)
    stacked = onehot.reshape(devices, ROW_DEV, EXPERTS)
    earlier = jnp.cumsum(stacked, axis=1) - stacked
    rank_within = jnp.sum(earlier * stacked, axis=2).reshape(-1).astype(jnp.int32)
    source = (jnp.arange(ROWS, dtype=jnp.int32) // ROW_DEV).astype(jnp.int32)
    slot_index = (choice_ids * per_expert + source * CAP + rank_within).astype(jnp.int32)
    out_grad = (route_weight[:, None] * cotangent.astype(jnp.float32)).astype(jnp.bfloat16)
    buffer_in = jnp.zeros((EXPERTS * per_expert, D), jnp.bfloat16).at[slot_index].set(routed_rows)
    buffer_grad = jnp.zeros((EXPERTS * per_expert, D), jnp.bfloat16).at[slot_index].set(out_grad)
    results = lax.map(expert_pass, (buffer_in.reshape(EXPERTS, per_expert, D),
                                    buffer_grad.reshape(EXPERTS, per_expert, D),
                                    gate_weight, up_weight, down_weight))
    expert_out, input_grad, gate_grad, up_grad, down_grad = results
    out_rows = expert_out.reshape(-1, D)[slot_index]
    row_grad = input_grad.reshape(-1, D)[slot_index]
    layer_out = (route_weight[:, None] * out_rows.astype(jnp.float32)).astype(jnp.bfloat16)
    weight_grad = jnp.sum(cotangent.astype(jnp.float32) * out_rows.astype(jnp.float32), axis=1)
    return layer_out, row_grad, weight_grad, gate_grad, up_grad, down_grad
```

```python
import functools

import jax
import jax.numpy as jnp
from jax import lax
from jax.experimental import pallas as pl
from jax.experimental.pallas import tpu as pltpu
from jax.sharding import PartitionSpec as P

CAP = 3
MAIN = 1536
TAIL = 512
WIDTH = MAIN + TAIL
PACK = 8
GROUP = 32
SLAB = PACK * GROUP
NT = (((1,), (1,)), ((), ()))
TN = (((0,), (0,)), ((), ()))


def iota(shape, dim):
    return lax.broadcasted_iota(jnp.int32, shape, dim)


def column_of(row, count):
    wide = jnp.broadcast_to(row, (count, count))
    return jnp.sum(
        jnp.where(iota((count, count), 0) == iota((count, count), 1), wide, 0.0),
        axis=1,
        keepdims=True,
    )


def slot_codes(index_row, count):
    expert = column_of(index_row, count)
    same = expert == jnp.broadcast_to(index_row, (count, count))
    before = iota((count, count), 1) < iota((count, count), 0)
    rank = jnp.sum(jnp.where(same & before, 1.0, 0.0), axis=1, keepdims=True)
    return 4.0 * expert + rank


def dispatch_kernel(index_ref, weight_ref, rows_ref, cot_ref, out_ref, right, codes):
    count = rows_ref.shape[0]
    step = pl.program_id(0)

    @pl.when(step == 0)
    def _():
        code = slot_codes(index_ref[...].astype(jnp.float32), count)
        shape = (count, 4 * count)
        lane = iota(shape, 1)
        part = (
            (lane >= count).astype(jnp.int32)
            + (lane >= 2 * count).astype(jnp.int32)
            + (lane >= 3 * count).astype(jnp.int32)
        )
        placed = code + 1024.0 * part.astype(jnp.float32)
        picked = jnp.where(iota(shape, 0) == lane - count * part, placed, 0.0)
        codes[...] = jnp.broadcast_to(jnp.sum(picked, axis=0, keepdims=True), codes.shape)
        weight = column_of(weight_ref[...], count)
        grad = (weight * cot_ref[...].astype(jnp.float32)).astype(jnp.bfloat16)
        rows = rows_ref[...]
        right[0:count, :] = rows[:, :MAIN]
        right[count : 2 * count, :] = grad[:, :MAIN]
        for rank in range(CAP):
            block = slice(TAIL * rank, TAIL * (rank + 1))
            right[2 * count : 3 * count, block] = rows[:, MAIN:]
            right[3 * count :, block] = grad[:, MAIN:]

    row = iota((SLAB, 1), 0)
    place = row & (PACK - 1)
    target = (GROUP * step + (row >> 3)) * 4
    lanes = codes[0:1, :]
    for rank in range(CAP):
        wanted = jnp.where(
            place < 3,
            target + place,
            jnp.where(
                place < 6,
                target + place + (1024 - 3),
                jnp.where(place == 6, target + (2048 + rank), target + (3072 + rank)),
            ),
        ).astype(jnp.float32)
        left = jnp.where(wanted == lanes, 1.0, 0.0).astype(jnp.bfloat16)
        block = slice(TAIL * rank, TAIL * (rank + 1))
        out_ref[:, block] = jnp.dot(
            left, right[:, block], preferred_element_type=jnp.float32
        ).astype(jnp.bfloat16)


def dispatch(index, weight, rows, cot, devices):
    count = rows.shape[0]
    return pl.pallas_call(
        dispatch_kernel,
        grid=(devices // GROUP,),
        in_specs=[
            pl.BlockSpec((1, count), lambda i: (0, 0)),
            pl.BlockSpec((1, count), lambda i: (0, 0)),
            pl.BlockSpec((count, WIDTH), lambda i: (0, 0)),
            pl.BlockSpec((count, WIDTH), lambda i: (0, 0)),
        ],
        out_specs=pl.BlockSpec((SLAB, MAIN), lambda i: (i, 0)),
        out_shape=jax.ShapeDtypeStruct((devices * PACK, MAIN), jnp.bfloat16),
        scratch_shapes=[
            pltpu.VMEM((4 * count, MAIN), jnp.bfloat16),
            pltpu.VMEM((8, 4 * count), jnp.float32),
        ],
        compiler_params=pltpu.CompilerParams(vmem_limit_bytes=24 << 20),
        name="dispatch",
    )(index, weight, rows, cot)


def split_matrix():
    out, packed = iota((SLAB, SLAB), 0), iota((SLAB, SLAB), 1)
    return jnp.where(packed == (out & (GROUP - 1)) * PACK + (out >> 5), 1.0, 0.0).astype(
        jnp.bfloat16
    )


def join_matrix():
    packed, out = iota((SLAB, SLAB), 0), iota((SLAB, SLAB), 1)
    return jnp.where(packed == (out & (GROUP - 1)) * PACK + (out >> 5), 1.0, 0.0).astype(
        jnp.bfloat16
    )


def unpack(packed, matrix, first, second, group):
    span = CAP * GROUP
    base = span * group
    for rank in range(CAP):
        block = slice(TAIL * rank, TAIL * (rank + 1))
        part = jnp.dot(matrix, packed[:, block], preferred_element_type=jnp.float32).astype(
            jnp.bfloat16
        )
        first[base : base + span, block] = part[0:span]
        second[base : base + span, block] = part[span : 2 * span]
        low = base + GROUP * rank
        first[low : low + GROUP, MAIN:] = part[2 * span : 2 * span + GROUP]
        second[low : low + GROUP, MAIN:] = part[2 * span + GROUP :]


def expert_kernel(
    got,
    w_gate,
    w_up,
    w_down,
    send,
    rows_out,
    grad_out,
    hidden_out,
    gate_out,
    up_out,
    packed,
    rows,
    grad,
    hidden,
    gate_pre,
    up_pre,
    result,
    input_grad,
    stacked,
    in_sem,
    out_sem,
    send_sem,
):
    groups = got.shape[0] // SLAB
    span = CAP * GROUP

    def load(group):
        part = pl.ds(SLAB * group, SLAB)
        return pltpu.make_async_copy(got.at[part], packed.at[part], in_sem.at[group])

    for group in range(groups):
        load(group).start()
    matrix = split_matrix()
    for group in range(groups):
        load(group).wait()
        unpack(packed.at[SLAB * group : SLAB * (group + 1)], matrix, rows, grad, group)
    saves = [pltpu.make_async_copy(rows, rows_out, out_sem.at[0])]
    saves.append(pltpu.make_async_copy(grad, grad_out, out_sem.at[1]))
    for save in saves:
        save.start()

    x = rows[...]
    gate_act = jnp.dot(x, w_gate[...], preferred_element_type=jnp.float32)
    up_act = jnp.dot(x, w_up[...], preferred_element_type=jnp.float32)
    hidden_grad = lax.dot_general(grad[...], w_down[...], NT, preferred_element_type=jnp.float32)
    sigma = jax.nn.sigmoid(gate_act)
    silu_gate = gate_act * sigma
    hidden[...] = (silu_gate * up_act).astype(jnp.bfloat16)
    gate_pre[...] = (hidden_grad * up_act * sigma * (1.0 + gate_act * (1.0 - sigma))).astype(
        jnp.bfloat16
    )
    up_pre[...] = (hidden_grad * silu_gate).astype(jnp.bfloat16)
    for number, (part, target) in enumerate(
        ((hidden, hidden_out), (gate_pre, gate_out), (up_pre, up_out))
    ):
        save = pltpu.make_async_copy(part, target, out_sem.at[2 + number])
        save.start()
        saves.append(save)
    result[...] = jnp.dot(hidden[...], w_down[...], preferred_element_type=jnp.float32).astype(
        jnp.bfloat16
    )
    input_grad[...] = (
        lax.dot_general(gate_pre[...], w_gate[...], NT, preferred_element_type=jnp.float32)
        + lax.dot_general(up_pre[...], w_up[...], NT, preferred_element_type=jnp.float32)
    ).astype(jnp.bfloat16)

    matrix = join_matrix()
    for group in range(groups):
        base = span * group
        stacked[0:span, :] = result[base : base + span, :MAIN]
        stacked[span : 2 * span, :] = input_grad[base : base + span, :MAIN]
        for rank in range(CAP):
            block = slice(TAIL * rank, TAIL * (rank + 1))
            low = base + GROUP * rank
            stacked[2 * span : 2 * span + GROUP, block] = result[low : low + GROUP, MAIN:]
            stacked[2 * span + GROUP :, block] = input_grad[low : low + GROUP, MAIN:]
        packed[SLAB * group : SLAB * (group + 1), :] = jnp.dot(
            matrix, stacked[...], preferred_element_type=jnp.float32
        ).astype(jnp.bfloat16)
        part = pl.ds(SLAB * group, SLAB)
        save = pltpu.make_async_copy(packed.at[part], send.at[part], send_sem.at[group])
        save.start()
        saves.append(save)
    for save in saves:
        save.wait()


def expert(got, w_gate, w_up, w_down):
    slots = got.shape[0] // PACK * CAP
    units = w_gate.shape[1]
    anywhere = pl.BlockSpec(memory_space=pl.ANY)
    local = pl.BlockSpec(memory_space=pltpu.VMEM)
    wide = jax.ShapeDtypeStruct((slots, WIDTH), jnp.bfloat16)
    narrow = jax.ShapeDtypeStruct((slots, units), jnp.bfloat16)
    groups = got.shape[0] // SLAB
    return pl.pallas_call(
        expert_kernel,
        in_specs=[anywhere, local, local, local],
        out_specs=[anywhere] * 6,
        out_shape=[
            jax.ShapeDtypeStruct(got.shape, jnp.bfloat16),
            wide,
            wide,
            narrow,
            narrow,
            narrow,
        ],
        scratch_shapes=[
            pltpu.VMEM(got.shape, jnp.bfloat16),
            pltpu.VMEM((slots, WIDTH), jnp.bfloat16),
            pltpu.VMEM((slots, WIDTH), jnp.bfloat16),
            pltpu.VMEM((slots, units), jnp.bfloat16),
            pltpu.VMEM((slots, units), jnp.bfloat16),
            pltpu.VMEM((slots, units), jnp.bfloat16),
            pltpu.VMEM((slots, WIDTH), jnp.bfloat16),
            pltpu.VMEM((slots, WIDTH), jnp.bfloat16),
            pltpu.VMEM((SLAB, MAIN), jnp.bfloat16),
            pltpu.SemaphoreType.DMA((groups,)),
            pltpu.SemaphoreType.DMA((5,)),
            pltpu.SemaphoreType.DMA((groups,)),
        ],
        compiler_params=pltpu.CompilerParams(vmem_limit_bytes=48 << 20),
        cost_estimate=pl.CostEstimate(
            flops=12 * slots * WIDTH * units,
            bytes_accessed=4 * got.size + 6 * WIDTH * units + 4 * slots * WIDTH,
            transcendentals=slots * units,
        ),
        name="expert",
    )(got, w_gate, w_up, w_down)


def combine_kernel(
    index_ref, weight_ref, cot_ref, got_ref, out_ref, row_ref, wgrad_ref, first, second, matrix
):
    count = cot_ref.shape[0]
    step = pl.program_id(0)
    groups = pl.num_programs(0)
    span = CAP * GROUP

    @pl.when(step == 0)
    def _():
        matrix[...] = split_matrix()

    base = pl.multiple_of(span * step, span)
    for rank in range(CAP):
        block = slice(TAIL * rank, TAIL * (rank + 1))
        part = jnp.dot(
            matrix[...], got_ref[:, block], preferred_element_type=jnp.float32
        ).astype(jnp.bfloat16)
        first[pl.ds(base, span), block] = part[0:span]
        second[pl.ds(base, span), block] = part[span : 2 * span]
        low = pl.multiple_of(base + GROUP * rank, GROUP)
        first[pl.ds(low, GROUP), MAIN:] = part[2 * span : 2 * span + GROUP]
        second[pl.ds(low, GROUP), MAIN:] = part[2 * span + GROUP :]

    @pl.when(step == groups - 1)
    def _():
        slots = first.shape[0]
        code = slot_codes(index_ref[...].astype(jnp.float32), count)
        lane = iota((count, slots), 1)
        group = jnp.zeros_like(lane)
        for edge in range(1, slots // span):
            group = group + (lane >= span * edge).astype(jnp.int32)
        inner = lane - span * group
        rank = (inner >= GROUP).astype(jnp.int32) + (inner >= 2 * GROUP).astype(jnp.int32)
        device = GROUP * group + inner - GROUP * rank
        pick = jnp.where(code == (4 * device + rank).astype(jnp.float32), 1.0, 0.0).astype(
            jnp.bfloat16
        )
        weight = column_of(weight_ref[...], count)
        total = jnp.zeros((count, 1), jnp.float32)
        for low in range(0, WIDTH, TAIL):
            block = slice(low, low + TAIL)
            out = jnp.dot(pick, first[:, block], preferred_element_type=jnp.float32)
            out_ref[:, block] = (weight * out).astype(jnp.bfloat16)
            total += jnp.sum(
                cot_ref[:, block].astype(jnp.float32) * out, axis=1, keepdims=True
            )
            row_ref[:, block] = jnp.dot(
                pick, second[:, block], preferred_element_type=jnp.float32
            ).astype(jnp.bfloat16)
        eye = iota((count, count), 0) == iota((count, count), 1)
        wgrad_ref[...] = jnp.sum(jnp.where(eye, total, 0.0), axis=0, keepdims=True)


def combine(index, weight, cot, got):
    count = cot.shape[0]
    groups = got.shape[0] // SLAB
    slots = groups * CAP * GROUP
    whole = lambda i: (0, 0)
    return pl.pallas_call(
        combine_kernel,
        grid=(groups,),
        in_specs=[
            pl.BlockSpec((1, count), whole),
            pl.BlockSpec((1, count), whole),
            pl.BlockSpec((count, WIDTH), whole),
            pl.BlockSpec((SLAB, MAIN), lambda i: (i, 0)),
        ],
        out_specs=[
            pl.BlockSpec((count, WIDTH), whole),
            pl.BlockSpec((count, WIDTH), whole),
            pl.BlockSpec((1, count), whole),
        ],
        out_shape=[
            jax.ShapeDtypeStruct((count, WIDTH), jnp.bfloat16),
            jax.ShapeDtypeStruct((count, WIDTH), jnp.bfloat16),
            jax.ShapeDtypeStruct((1, count), jnp.float32),
        ],
        scratch_shapes=[
            pltpu.VMEM((slots, WIDTH), jnp.bfloat16),
            pltpu.VMEM((slots, WIDTH), jnp.bfloat16),
            pltpu.VMEM((SLAB, SLAB), jnp.bfloat16),
        ],
        compiler_params=pltpu.CompilerParams(vmem_limit_bytes=24 << 20),
        name="combine",
    )(index, weight, cot, got)


def exchange(packed, devices):
    moved = lax.all_to_all(
        packed.reshape(devices, PACK, MAIN), "expert", split_axis=0, concat_axis=0, tiled=True
    )
    return moved.reshape(packed.shape)


def weight_product(left, right):
    return lax.dot_general(left, right, TN, preferred_element_type=jnp.float32).astype(
        jnp.bfloat16
    )


def local(routed_rows, expert_index, route_weight, cotangent, gate_weight, up_weight, down_weight):
    devices = lax.axis_size("expert")
    count = routed_rows.shape[0]
    index = expert_index.reshape(1, count)
    weight = route_weight.reshape(1, count)
    packed = dispatch(index, weight, routed_rows, cotangent, devices)
    got = exchange(packed, devices)
    send, rows, grad, hidden, gate_pre, up_pre = expert(
        got, gate_weight[0], up_weight[0], down_weight[0]
    )
    back = exchange(send, devices)
    gate_grad = weight_product(rows, gate_pre)
    up_grad = weight_product(rows, up_pre)
    down_grad = weight_product(hidden, grad)
    layer_out, row_grad, weight_grad = combine(index, weight, cotangent, back)
    return (
        layer_out,
        row_grad,
        weight_grad.reshape(count),
        gate_grad[None],
        up_grad[None],
        down_grad[None],
    )


def solution(mesh):
    rows = P("expert", None)
    weights = P("expert", None, None)
    return jax.shard_map(
        local,
        mesh=mesh,
        in_specs=(rows, rows, P("expert"), rows, weights, weights, weights),
        out_specs=(rows, rows, P("expert"), weights, weights, weights),
        check_vma=False,
    )
```

```python
import functools

import jax
import jax.numpy as jnp
from jax import lax
from jax.experimental import pallas as pl
from jax.experimental.pallas import tpu as pltpu
from jax.sharding import PartitionSpec as P

CAP = 3
MAIN = 1536
TAIL = 512
WIDTH = MAIN + TAIL
PACK = 8
GROUP = 32
SLAB = PACK * GROUP
NT = (((1,), (1,)), ((), ()))
TN = (((0,), (0,)), ((), ()))


def iota(shape, dim):
    return lax.broadcasted_iota(jnp.int32, shape, dim)


def column_of(row, count):
    wide = jnp.broadcast_to(row, (count, count))
    return jnp.sum(
        jnp.where(iota((count, count), 0) == iota((count, count), 1), wide, 0.0),
        axis=1,
        keepdims=True,
    )


def slot_codes(index_row, count):
    expert = column_of(index_row, count)
    same = expert == jnp.broadcast_to(index_row, (count, count))
    before = iota((count, count), 1) < iota((count, count), 0)
    rank = jnp.sum(jnp.where(same & before, 1.0, 0.0), axis=1, keepdims=True)
    return 4.0 * expert + rank


def dispatch_kernel(
    index_hbm, weight_hbm, rows_hbm, cot_hbm, out_ref, index, weight, rows, cot, right, in_sem
):
    count = rows.shape[0]
    loads = [
        pltpu.make_async_copy(source, target, in_sem.at[number])
        for number, (source, target) in enumerate(
            ((index_hbm, index), (weight_hbm, weight), (rows_hbm, rows), (cot_hbm, cot))
        )
    ]
    for load in loads:
        load.start()
    loads[0].wait()
    code = slot_codes(index[...].astype(jnp.float32), count)
    shape = (count, 4 * count)
    lane = iota(shape, 1)
    part = (
        (lane >= count).astype(jnp.int32)
        + (lane >= 2 * count).astype(jnp.int32)
        + (lane >= 3 * count).astype(jnp.int32)
    )
    placed = code + 1024.0 * part.astype(jnp.float32)
    picked = jnp.where(iota(shape, 0) == lane - count * part, placed, 0.0)
    lanes = jnp.sum(picked, axis=0, keepdims=True)
    loads[1].wait()
    scale = column_of(weight[...], count)
    loads[2].wait()
    right[0:count, :] = rows[:, :MAIN]
    for rank in range(CAP):
        right[2 * count : 3 * count, TAIL * rank : TAIL * (rank + 1)] = rows[:, MAIN:]
    loads[3].wait()
    grad = (scale * cot[...].astype(jnp.float32)).astype(jnp.bfloat16)
    right[count : 2 * count, :] = grad[:, :MAIN]
    for rank in range(CAP):
        right[3 * count :, TAIL * rank : TAIL * (rank + 1)] = grad[:, MAIN:]

    row = iota((SLAB, 1), 0)
    place = row & (PACK - 1)
    for group in range(out_ref.shape[0] // SLAB):
        target = (GROUP * group + (row >> 3)) * 4
        for rank in range(CAP):
            wanted = jnp.where(
                place < 3,
                target + place,
                jnp.where(
                    place < 6,
                    target + place + (1024 - 3),
                    jnp.where(place == 6, target + (2048 + rank), target + (3072 + rank)),
                ),
            ).astype(jnp.float32)
            left = jnp.where(wanted == lanes, 1.0, 0.0).astype(jnp.bfloat16)
            block = slice(TAIL * rank, TAIL * (rank + 1))
            out_ref[SLAB * group : SLAB * (group + 1), block] = jnp.dot(
                left, right[:, block], preferred_element_type=jnp.float32
            ).astype(jnp.bfloat16)


def in_hbm(array):
    return pltpu.with_memory_space_constraint(array, pltpu.HBM)


def in_vmem(array):
    return pltpu.with_memory_space_constraint(array, pltpu.VMEM)


ANYWHERE = pl.BlockSpec(memory_space=pl.ANY)
LOCAL = pl.BlockSpec(memory_space=pltpu.VMEM)


def dispatch(index, weight, rows, cot, devices):
    count = rows.shape[0]
    return pl.pallas_call(
        dispatch_kernel,
        in_specs=[ANYWHERE] * 4,
        out_specs=LOCAL,
        out_shape=pltpu.VMEM((devices * PACK, MAIN), jnp.bfloat16),
        scratch_shapes=[
            pltpu.VMEM((1, count), jnp.int32),
            pltpu.VMEM((1, count), jnp.float32),
            pltpu.VMEM((count, WIDTH), jnp.bfloat16),
            pltpu.VMEM((count, WIDTH), jnp.bfloat16),
            pltpu.VMEM((4 * count, MAIN), jnp.bfloat16),
            pltpu.SemaphoreType.DMA((4,)),
        ],
        compiler_params=pltpu.CompilerParams(vmem_limit_bytes=24 << 20),
        name="dispatch",
    )(in_hbm(index), in_hbm(weight), in_hbm(rows), in_hbm(cot))


def split_matrix():
    out, packed = iota((SLAB, SLAB), 0), iota((SLAB, SLAB), 1)
    return jnp.where(packed == (out & (GROUP - 1)) * PACK + (out >> 5), 1.0, 0.0).astype(
        jnp.bfloat16
    )


def join_matrix():
    packed, out = iota((SLAB, SLAB), 0), iota((SLAB, SLAB), 1)
    return jnp.where(packed == (out & (GROUP - 1)) * PACK + (out >> 5), 1.0, 0.0).astype(
        jnp.bfloat16
    )


def unpack(packed, matrix, first, second, group):
    span = CAP * GROUP
    base = span * group
    for rank in range(CAP):
        block = slice(TAIL * rank, TAIL * (rank + 1))
        part = jnp.dot(matrix, packed[:, block], preferred_element_type=jnp.float32).astype(
            jnp.bfloat16
        )
        first[base : base + span, block] = part[0:span]
        second[base : base + span, block] = part[span : 2 * span]
        low = base + GROUP * rank
        first[low : low + GROUP, MAIN:] = part[2 * span : 2 * span + GROUP]
        second[low : low + GROUP, MAIN:] = part[2 * span + GROUP :]


def expert_kernel(
    got,
    w_gate,
    w_up,
    w_down,
    send,
    rows_out,
    grad_out,
    hidden_out,
    gate_out,
    up_out,
    packed,
    rows,
    grad,
    hidden,
    gate_pre,
    up_pre,
    result,
    input_grad,
    stacked,
    out_sem,
    send_sem,
):
    groups = got.shape[0] // SLAB
    span = CAP * GROUP

    matrix = split_matrix()
    for group in range(groups):
        unpack(got.at[SLAB * group : SLAB * (group + 1)], matrix, rows, grad, group)
    saves = [pltpu.make_async_copy(rows, rows_out, out_sem.at[0])]
    saves.append(pltpu.make_async_copy(grad, grad_out, out_sem.at[1]))
    for save in saves:
        save.start()

    x = rows[...]
    gate_act = jnp.dot(x, w_gate[...], preferred_element_type=jnp.float32)
    up_act = jnp.dot(x, w_up[...], preferred_element_type=jnp.float32)
    hidden_grad = lax.dot_general(grad[...], w_down[...], NT, preferred_element_type=jnp.float32)
    sigma = jax.nn.sigmoid(gate_act)
    silu_gate = gate_act * sigma
    hidden[...] = (silu_gate * up_act).astype(jnp.bfloat16)
    gate_pre[...] = (hidden_grad * up_act * sigma * (1.0 + gate_act * (1.0 - sigma))).astype(
        jnp.bfloat16
    )
    up_pre[...] = (hidden_grad * silu_gate).astype(jnp.bfloat16)
    for number, (part, target) in enumerate(
        ((hidden, hidden_out), (gate_pre, gate_out), (up_pre, up_out))
    ):
        save = pltpu.make_async_copy(part, target, out_sem.at[2 + number])
        save.start()
        saves.append(save)
    result[...] = jnp.dot(hidden[...], w_down[...], preferred_element_type=jnp.float32).astype(
        jnp.bfloat16
    )
    input_grad[...] = (
        lax.dot_general(gate_pre[...], w_gate[...], NT, preferred_element_type=jnp.float32)
        + lax.dot_general(up_pre[...], w_up[...], NT, preferred_element_type=jnp.float32)
    ).astype(jnp.bfloat16)

    matrix = join_matrix()
    for group in range(groups):
        base = span * group
        stacked[0:span, :] = result[base : base + span, :MAIN]
        stacked[span : 2 * span, :] = input_grad[base : base + span, :MAIN]
        for rank in range(CAP):
            block = slice(TAIL * rank, TAIL * (rank + 1))
            low = base + GROUP * rank
            stacked[2 * span : 2 * span + GROUP, block] = result[low : low + GROUP, MAIN:]
            stacked[2 * span + GROUP :, block] = input_grad[low : low + GROUP, MAIN:]
        packed[SLAB * group : SLAB * (group + 1), :] = jnp.dot(
            matrix, stacked[...], preferred_element_type=jnp.float32
        ).astype(jnp.bfloat16)
        part = pl.ds(SLAB * group, SLAB)
        save = pltpu.make_async_copy(packed.at[part], send.at[part], send_sem.at[group])
        save.start()
        saves.append(save)
    for save in saves:
        save.wait()


def expert(got, w_gate, w_up, w_down):
    slots = got.shape[0] // PACK * CAP
    units = w_gate.shape[1]
    wide = pltpu.HBM((slots, WIDTH), jnp.bfloat16)
    narrow = pltpu.HBM((slots, units), jnp.bfloat16)
    groups = got.shape[0] // SLAB
    return pl.pallas_call(
        expert_kernel,
        in_specs=[LOCAL] * 4,
        out_specs=[ANYWHERE] * 6,
        out_shape=[
            pltpu.HBM(got.shape, jnp.bfloat16),
            wide,
            wide,
            narrow,
            narrow,
            narrow,
        ],
        scratch_shapes=[
            pltpu.VMEM(got.shape, jnp.bfloat16),
            pltpu.VMEM((slots, WIDTH), jnp.bfloat16),
            pltpu.VMEM((slots, WIDTH), jnp.bfloat16),
            pltpu.VMEM((slots, units), jnp.bfloat16),
            pltpu.VMEM((slots, units), jnp.bfloat16),
            pltpu.VMEM((slots, units), jnp.bfloat16),
            pltpu.VMEM((slots, WIDTH), jnp.bfloat16),
            pltpu.VMEM((slots, WIDTH), jnp.bfloat16),
            pltpu.VMEM((SLAB, MAIN), jnp.bfloat16),
            pltpu.SemaphoreType.DMA((5,)),
            pltpu.SemaphoreType.DMA((groups,)),
        ],
        compiler_params=pltpu.CompilerParams(vmem_limit_bytes=48 << 20),
        cost_estimate=pl.CostEstimate(
            flops=12 * slots * WIDTH * units,
            bytes_accessed=4 * got.size + 6 * WIDTH * units + 4 * slots * WIDTH,
            transcendentals=slots * units,
        ),
        name="expert",
    )(in_vmem(got), in_vmem(w_gate), in_vmem(w_up), in_vmem(w_down))


def combine_kernel(
    index_hbm,
    weight_hbm,
    cot_hbm,
    got,
    out_hbm,
    row_hbm,
    wgrad_ref,
    index,
    weight,
    cot,
    first,
    second,
    out,
    row,
    in_sem,
    out_sem,
):
    count = cot.shape[0]
    slots = first.shape[0]
    span = CAP * GROUP
    loads = [
        pltpu.make_async_copy(source, target, in_sem.at[number])
        for number, (source, target) in enumerate(
            ((index_hbm, index), (weight_hbm, weight), (cot_hbm, cot))
        )
    ]
    for load in loads:
        load.start()
    matrix = split_matrix()
    for group in range(got.shape[0] // SLAB):
        unpack(got.at[SLAB * group : SLAB * (group + 1)], matrix, first, second, group)
    loads[0].wait()
    code = slot_codes(index[...].astype(jnp.float32), count)
    lane = iota((count, slots), 1)
    group = jnp.zeros_like(lane)
    for edge in range(1, slots // span):
        group = group + (lane >= span * edge).astype(jnp.int32)
    inner = lane - span * group
    rank = (inner >= GROUP).astype(jnp.int32) + (inner >= 2 * GROUP).astype(jnp.int32)
    device = GROUP * group + inner - GROUP * rank
    pick = jnp.where(code == (4 * device + rank).astype(jnp.float32), 1.0, 0.0).astype(
        jnp.bfloat16
    )
    loads[1].wait()
    scale = column_of(weight[...], count)
    loads[2].wait()
    total = jnp.zeros((count, 1), jnp.float32)
    saves = []

    def save(source, target):
        copy = pltpu.make_async_copy(source, target, out_sem.at[len(saves)])
        copy.start()
        saves.append(copy)

    for low in range(0, WIDTH, TAIL):
        block = slice(low, low + TAIL)
        value = jnp.dot(pick, first[:, block], preferred_element_type=jnp.float32)
        out[:, block] = (scale * value).astype(jnp.bfloat16)
        save(out.at[:, block], out_hbm.at[:, block])
        total += jnp.sum(cot[:, block].astype(jnp.float32) * value, axis=1, keepdims=True)
        row[:, block] = jnp.dot(
            pick, second[:, block], preferred_element_type=jnp.float32
        ).astype(jnp.bfloat16)
        save(row.at[:, block], row_hbm.at[:, block])
    eye = iota((count, count), 0) == iota((count, count), 1)
    wgrad_ref[...] = jnp.sum(jnp.where(eye, total, 0.0), axis=0, keepdims=True)
    for copy in saves:
        copy.wait()


def combine(index, weight, cot, got):
    count = cot.shape[0]
    slots = got.shape[0] // PACK * CAP
    return pl.pallas_call(
        combine_kernel,
        in_specs=[ANYWHERE, ANYWHERE, ANYWHERE, LOCAL],
        out_specs=[ANYWHERE, ANYWHERE, LOCAL],
        out_shape=[
            pltpu.HBM((count, WIDTH), jnp.bfloat16),
            pltpu.HBM((count, WIDTH), jnp.bfloat16),
            jax.ShapeDtypeStruct((1, count), jnp.float32),
        ],
        scratch_shapes=[
            pltpu.VMEM((1, count), jnp.int32),
            pltpu.VMEM((1, count), jnp.float32),
            pltpu.VMEM((count, WIDTH), jnp.bfloat16),
            pltpu.VMEM((slots, WIDTH), jnp.bfloat16),
            pltpu.VMEM((slots, WIDTH), jnp.bfloat16),
            pltpu.VMEM((count, WIDTH), jnp.bfloat16),
            pltpu.VMEM((count, WIDTH), jnp.bfloat16),
            pltpu.SemaphoreType.DMA((3,)),
            pltpu.SemaphoreType.DMA((2 * WIDTH // TAIL,)),
        ],
        compiler_params=pltpu.CompilerParams(vmem_limit_bytes=24 << 20),
        name="combine",
    )(in_hbm(index), in_hbm(weight), in_hbm(cot), in_vmem(got))


def exchange(packed, devices):
    moved = lax.all_to_all(
        packed.reshape(devices, PACK, MAIN), "expert", split_axis=0, concat_axis=0, tiled=True
    )
    return moved.reshape(packed.shape)


def weight_product(left, right):
    return lax.dot_general(left, right, TN, preferred_element_type=jnp.float32).astype(
        jnp.bfloat16
    )


def local(routed_rows, expert_index, route_weight, cotangent, gate_weight, up_weight, down_weight):
    devices = lax.axis_size("expert")
    count = routed_rows.shape[0]
    index = expert_index.reshape(1, count)
    weight = route_weight.reshape(1, count)
    packed = dispatch(index, weight, routed_rows, cotangent, devices)
    got = exchange(packed, devices)
    send, rows, grad, hidden, gate_pre, up_pre = expert(
        got, gate_weight[0], up_weight[0], down_weight[0]
    )
    back = exchange(send, devices)
    gate_grad = weight_product(rows, gate_pre)
    up_grad = weight_product(rows, up_pre)
    down_grad = weight_product(hidden, grad)
    layer_out, row_grad, weight_grad = combine(index, weight, cotangent, back)
    return (
        layer_out,
        row_grad,
        weight_grad.reshape(count),
        gate_grad[None],
        up_grad[None],
        down_grad[None],
    )


def solution(mesh):
    rows = P("expert", None)
    weights = P("expert", None, None)
    return jax.shard_map(
        local,
        mesh=mesh,
        in_specs=(rows, rows, P("expert"), rows, weights, weights, weights),
        out_specs=(rows, rows, P("expert"), weights, weights, weights),
        check_vma=False,
    )
```

```python
import jax
import jax.numpy as jnp
from jax import lax
from jax.experimental import pallas as pl
from jax.experimental.pallas import tpu as pltpu
from jax.sharding import PartitionSpec as P

CAP = 3
MAIN = 1536
TAIL = 512
WIDTH = MAIN + TAIL
PACK = 8
GROUP = 32
SLAB = PACK * GROUP
SPAN = CAP * GROUP
NT = (((1,), (1,)), ((), ()))
TN = (((0,), (0,)), ((), ()))
ANYWHERE = pl.BlockSpec(memory_space=pl.ANY)
LOCAL = pl.BlockSpec(memory_space=pltpu.VMEM)


def in_hbm(array):
    return pltpu.with_memory_space_constraint(array, pltpu.HBM)


def in_vmem(array):
    return pltpu.with_memory_space_constraint(array, pltpu.VMEM)


def iota(shape, dim):
    return lax.broadcasted_iota(jnp.int32, shape, dim)


def dot(left, right):
    return jnp.dot(left, right, preferred_element_type=jnp.float32)


def column_of(row, count):
    wide = jnp.broadcast_to(row, (count, count))
    return jnp.sum(
        jnp.where(iota((count, count), 0) == iota((count, count), 1), wide, 0.0),
        axis=1,
        keepdims=True,
    )


def ranks(index_row, count, axis):
    expert = column_of(index_row, count)
    same = expert == jnp.broadcast_to(index_row, (count, count))
    first, second = iota((count, count), axis), iota((count, count), 1 - axis)
    found = jnp.sum(jnp.where(same & (first < second), 1.0, 0.0), axis=axis, keepdims=True)
    return found, expert


def slot_code(shape, dim):
    slot = iota(shape, dim)
    group = jnp.zeros_like(slot)
    for edge in range(1, shape[dim] // SPAN):
        group = group + (slot >= SPAN * edge).astype(jnp.int32)
    inner = slot - SPAN * group
    rank = (inner >= GROUP).astype(jnp.int32) + (inner >= 2 * GROUP).astype(jnp.int32)
    return (4 * (GROUP * group + inner - GROUP * rank) + rank).astype(jnp.float32)


def split_matrix():
    out, packed = iota((SLAB, SLAB), 0), iota((SLAB, SLAB), 1)
    match = packed == (out & (GROUP - 1)) * PACK + (out >> 5)
    return jnp.where(match, 1.0, 0.0).astype(jnp.bfloat16)


def join_matrix():
    packed, out = iota((SLAB, SLAB), 0), iota((SLAB, SLAB), 1)
    match = packed == (out & (GROUP - 1)) * PACK + (out >> 5)
    return jnp.where(match, 1.0, 0.0).astype(jnp.bfloat16)


def store_stacked(stacked, value, low, which):
    value = value.astype(jnp.bfloat16)
    width = value.shape[1]
    for group in range(value.shape[0] // SPAN):
        base = SLAB * group
        if low < MAIN:
            stacked[base + SPAN * which : base + SPAN * (which + 1), low : low + width] = value[
                SPAN * group : SPAN * (group + 1)
            ]
        else:
            tail = base + 2 * SPAN + GROUP * which
            for rank in range(CAP):
                start = SPAN * group + GROUP * rank
                column = TAIL * rank + low - MAIN
                stacked[tail : tail + GROUP, column : column + width] = value[
                    start : start + GROUP
                ]


def pack(out, stacked):
    matrix = join_matrix()
    for group in range(out.shape[0] // SLAB):
        part = slice(SLAB * group, SLAB * (group + 1))
        for low in range(0, MAIN, TAIL):
            block = slice(low, low + TAIL)
            out[part, block] = dot(matrix, stacked[part, block]).astype(jnp.bfloat16)


def unpack(packed, matrix, first, second, group):
    base = SPAN * group
    for rank in range(CAP):
        block = slice(TAIL * rank, TAIL * (rank + 1))
        part = dot(matrix, packed[SLAB * group : SLAB * (group + 1), block]).astype(jnp.bfloat16)
        first[base : base + SPAN, block] = part[0:SPAN]
        second[base : base + SPAN, block] = part[SPAN : 2 * SPAN]
        low = base + GROUP * rank
        first[low : low + GROUP, MAIN:] = part[2 * SPAN : 2 * SPAN + GROUP]
        second[low : low + GROUP, MAIN:] = part[2 * SPAN + GROUP :]


def dispatch_kernel(
    index_hbm, weight_hbm, rows_hbm, cot_hbm, out, index, weight, rows, cot, stacked, in_sem
):
    count = rows.shape[0]
    slots = out.shape[0] // PACK * CAP
    loads = [
        pltpu.make_async_copy(source, target, in_sem.at[number])
        for number, (source, target) in enumerate(
            ((index_hbm, index), (weight_hbm, weight), (rows_hbm, rows), (cot_hbm, cot))
        )
    ]
    for load in loads:
        load.start()
    loads[0].wait()
    index_row = index[...].astype(jnp.float32)
    rank_row, _ = ranks(index_row, count, 0)
    place = jnp.where(slot_code((slots, 1), 0) == 4.0 * index_row + rank_row, 1.0, 0.0).astype(
        jnp.bfloat16
    )
    loads[1].wait()
    scale = column_of(weight[...], count)
    loads[2].wait()
    for low in range(0, WIDTH, TAIL):
        store_stacked(stacked, dot(place, rows[:, low : low + TAIL]), low, 0)
    loads[3].wait()
    for low in range(0, WIDTH, TAIL):
        grad = (scale * cot[:, low : low + TAIL].astype(jnp.float32)).astype(jnp.bfloat16)
        store_stacked(stacked, dot(place, grad), low, 1)
    pack(out, stacked)


def dispatch(index, weight, rows, cot, devices):
    count = rows.shape[0]
    return pl.pallas_call(
        dispatch_kernel,
        in_specs=[ANYWHERE] * 4,
        out_specs=LOCAL,
        out_shape=pltpu.VMEM((devices * PACK, MAIN), jnp.bfloat16),
        scratch_shapes=[
            pltpu.VMEM((1, count), jnp.int32),
            pltpu.VMEM((1, count), jnp.float32),
            pltpu.VMEM((count, WIDTH), jnp.bfloat16),
            pltpu.VMEM((count, WIDTH), jnp.bfloat16),
            pltpu.VMEM((devices * PACK, MAIN), jnp.bfloat16),
            pltpu.SemaphoreType.DMA((4,)),
        ],
        compiler_params=pltpu.CompilerParams(vmem_limit_bytes=24 << 20),
        name="dispatch",
    )(in_hbm(index), in_hbm(weight), in_hbm(rows), in_hbm(cot))


def saver(semaphores):
    saves = []

    def save(source, target):
        copy = pltpu.make_async_copy(source, target, semaphores.at[len(saves)])
        copy.start()
        saves.append(copy)

    return save, saves


def expert_kernel(
    got,
    w_gate,
    w_up,
    w_down,
    send_hbm,
    rows_hbm,
    grad_hbm,
    hidden_hbm,
    gate_hbm,
    up_hbm,
    send,
    rows,
    grad,
    hidden,
    gate_pre,
    up_pre,
    stacked,
    out_sem,
):
    save, saves = saver(out_sem)
    groups = got.shape[0] // SLAB
    matrix, join = split_matrix(), join_matrix()
    for group in range(groups):
        unpack(got, matrix, rows, grad, group)
    save(rows, rows_hbm)
    save(grad, grad_hbm)

    gate_act = dot(rows[...], w_gate[...])
    up_act = dot(rows[...], w_up[...])
    hidden_grad = lax.dot_general(
        grad[...], w_down[...], NT, preferred_element_type=jnp.float32
    )
    sigma = jax.nn.sigmoid(gate_act)
    silu_gate = gate_act * sigma
    hidden[...] = (silu_gate * up_act).astype(jnp.bfloat16)
    gate_pre[...] = (
        hidden_grad * up_act * sigma * (1.0 + gate_act * (1.0 - sigma))
    ).astype(jnp.bfloat16)
    up_pre[...] = (hidden_grad * silu_gate).astype(jnp.bfloat16)
    save(hidden, hidden_hbm)
    save(gate_pre, gate_hbm)
    save(up_pre, up_hbm)

    def project(low):
        block = slice(low, low + TAIL)
        store_stacked(stacked, dot(hidden[...], w_down[:, block]), low, 0)
        value = lax.dot_general(
            gate_pre[...], w_gate[block, :], NT, preferred_element_type=jnp.float32
        ) + lax.dot_general(
            up_pre[...], w_up[block, :], NT, preferred_element_type=jnp.float32
        )
        store_stacked(stacked, value, low, 1)

    project(MAIN)
    for rank in range(CAP):
        project(TAIL * rank)
        block = slice(TAIL * rank, TAIL * (rank + 1))
        for group in range(groups):
            part = slice(SLAB * group, SLAB * (group + 1))
            send[part, block] = dot(join, stacked[part, block]).astype(jnp.bfloat16)
        save(send.at[:, block], send_hbm.at[:, block])
    for copy in saves:
        copy.wait()


def expert(got, w_gate, w_up, w_down):
    slots = got.shape[0] // PACK * CAP
    units = w_gate.shape[1]
    shapes = [got.shape] + [(slots, WIDTH)] * 2 + [(slots, units)] * 3
    return pl.pallas_call(
        expert_kernel,
        in_specs=[LOCAL] * 4,
        out_specs=[ANYWHERE] * 6,
        out_shape=[pltpu.HBM(shape, jnp.bfloat16) for shape in shapes],
        scratch_shapes=[pltpu.VMEM(shape, jnp.bfloat16) for shape in shapes]
        + [
            pltpu.VMEM(got.shape, jnp.bfloat16),
            pltpu.SemaphoreType.DMA((5 + CAP,)),
        ],
        compiler_params=pltpu.CompilerParams(vmem_limit_bytes=40 << 20),
        cost_estimate=pl.CostEstimate(
            flops=12 * slots * WIDTH * units,
            bytes_accessed=4 * got.size + 6 * WIDTH * units + 4 * slots * WIDTH,
            transcendentals=slots * units,
        ),
        name="expert",
    )(in_vmem(got), in_vmem(w_gate), in_vmem(w_up), in_vmem(w_down))


def gradient_kernel(
    index,
    weight,
    rows,
    grad,
    hidden,
    gate_pre,
    up_pre,
    gate_hbm,
    up_hbm,
    down_hbm,
    pick,
    scale,
    gate_grad,
    up_grad,
    down_grad,
    out_sem,
):
    count = index.shape[1]
    slots = rows.shape[0]
    save, saves = saver(out_sem)

    for left, right, result, target in (
        (rows, gate_pre, gate_grad, gate_hbm),
        (rows, up_pre, up_grad, up_hbm),
        (hidden, grad, down_grad, down_hbm),
    ):
        for low in range(0, left.shape[1], 256):
            block = slice(low, low + 256)
            result[block, :] = lax.dot_general(
                left[:, block], right[...], TN, preferred_element_type=jnp.float32
            ).astype(jnp.bfloat16)
        save(result, target)
    rank, expert_column = ranks(index[...].astype(jnp.float32), count, 1)
    code = 4.0 * expert_column + rank
    pick[...] = jnp.where(code == slot_code((1, slots), 1), 1.0, 0.0).astype(jnp.bfloat16)
    scale[...] = jnp.broadcast_to(column_of(weight[...], count), scale.shape)
    for copy in saves:
        copy.wait()


def gradients(index, weight, rows, grad, hidden, gate_pre, up_pre):
    count = index.shape[1]
    slots, units = hidden.shape
    tall = (WIDTH, units)
    flat = (units, WIDTH)
    return pl.pallas_call(
        gradient_kernel,
        in_specs=[LOCAL] * 7,
        out_specs=[ANYWHERE] * 3 + [LOCAL] * 2,
        out_shape=[
            pltpu.HBM(tall, jnp.bfloat16),
            pltpu.HBM(tall, jnp.bfloat16),
            pltpu.HBM(flat, jnp.bfloat16),
            pltpu.VMEM((count, slots), jnp.bfloat16),
            pltpu.VMEM((count, 128), jnp.float32),
        ],
        scratch_shapes=[
            pltpu.VMEM(tall, jnp.bfloat16),
            pltpu.VMEM(tall, jnp.bfloat16),
            pltpu.VMEM(flat, jnp.bfloat16),
            pltpu.SemaphoreType.DMA((3,)),
        ],
        compiler_params=pltpu.CompilerParams(vmem_limit_bytes=40 << 20),
        cost_estimate=pl.CostEstimate(
            flops=6 * slots * WIDTH * units,
            bytes_accessed=6 * WIDTH * units + 4 * slots * WIDTH,
            transcendentals=0,
        ),
        name="gradients",
    )(
        in_hbm(index),
        in_hbm(weight),
        in_hbm(rows),
        in_hbm(grad),
        in_hbm(hidden),
        in_hbm(gate_pre),
        in_hbm(up_pre),
    )


def combine_kernel(
    pick,
    scale,
    cot_hbm,
    got,
    out_hbm,
    row_hbm,
    wgrad_hbm,
    cot,
    first,
    second,
    out,
    row,
    wgrad,
    in_sem,
    out_sem,
):
    count = cot.shape[0]
    load = pltpu.make_async_copy(cot_hbm, cot, in_sem)
    load.start()
    matrix = split_matrix()
    for group in range(got.shape[0] // SLAB):
        unpack(got, matrix, first, second, group)
    save, saves = saver(out_sem)
    factor = scale[:, 0:1]
    total = jnp.zeros((count, 1), jnp.float32)

    def store_rows(block):
        row[:, block] = dot(pick[...], second[:, block]).astype(jnp.bfloat16)
        save(row.at[:, block], row_hbm.at[:, block])

    blocks = [slice(low, low + TAIL) for low in range(0, WIDTH, TAIL)]
    for block in blocks:
        if block != blocks[-1]:
            store_rows(block)
        value = dot(pick[...], first[:, block])
        out[:, block] = (factor * value).astype(jnp.bfloat16)
        save(out.at[:, block], out_hbm.at[:, block])
        if block == blocks[0]:
            load.wait()
        total += jnp.sum(cot[:, block].astype(jnp.float32) * value, axis=1, keepdims=True)
    eye = iota((count, count), 0) == iota((count, count), 1)
    wgrad[...] = jnp.sum(jnp.where(eye, total, 0.0), axis=0, keepdims=True)
    save(wgrad, wgrad_hbm)
    store_rows(blocks[-1])
    for copy in saves:
        copy.wait()


def combine(pick, scale, cot, got):
    count = cot.shape[0]
    slots = got.shape[0] // PACK * CAP
    return pl.pallas_call(
        combine_kernel,
        in_specs=[LOCAL, LOCAL, ANYWHERE, LOCAL],
        out_specs=[ANYWHERE] * 3,
        out_shape=[
            pltpu.HBM((count, WIDTH), jnp.bfloat16),
            pltpu.HBM((count, WIDTH), jnp.bfloat16),
            pltpu.HBM((1, count), jnp.float32),
        ],
        scratch_shapes=[
            pltpu.VMEM((count, WIDTH), jnp.bfloat16),
            pltpu.VMEM((slots, WIDTH), jnp.bfloat16),
            pltpu.VMEM((slots, WIDTH), jnp.bfloat16),
            pltpu.VMEM((count, WIDTH), jnp.bfloat16),
            pltpu.VMEM((count, WIDTH), jnp.bfloat16),
            pltpu.VMEM((1, count), jnp.float32),
            pltpu.SemaphoreType.DMA,
            pltpu.SemaphoreType.DMA((2 * WIDTH // TAIL + 1,)),
        ],
        compiler_params=pltpu.CompilerParams(vmem_limit_bytes=24 << 20),
        name="combine",
    )(in_vmem(pick), in_vmem(scale), in_hbm(cot), in_vmem(got))


def exchange(packed, devices):
    moved = lax.all_to_all(
        packed.reshape(devices, PACK, MAIN), "expert", split_axis=0, concat_axis=0, tiled=True
    )
    return moved.reshape(packed.shape)


def local(routed_rows, expert_index, route_weight, cotangent, gate_weight, up_weight, down_weight):
    devices = lax.axis_size("expert")
    count = routed_rows.shape[0]
    index = expert_index.reshape(1, count)
    weight = route_weight.reshape(1, count)
    packed = dispatch(index, weight, routed_rows, cotangent, devices)
    got = exchange(packed, devices)
    send, *saved = expert(got, gate_weight[0], up_weight[0], down_weight[0])
    back = exchange(send, devices)
    gate_grad, up_grad, down_grad, pick, scale = gradients(index, weight, *saved)
    layer_out, row_grad, weight_grad = combine(pick, scale, cotangent, back)
    return (
        layer_out,
        row_grad,
        weight_grad.reshape(count),
        gate_grad[None],
        up_grad[None],
        down_grad[None],
    )


def solution(mesh):
    rows = P("expert", None)
    weights = P("expert", None, None)
    return jax.shard_map(
        local,
        mesh=mesh,
        in_specs=(rows, rows, P("expert"), rows, weights, weights, weights),
        out_specs=(rows, rows, P("expert"), weights, weights, weights),
        check_vma=False,
    )
```

```python
import jax
import jax.numpy as jnp
from jax import lax
from jax.experimental import pallas as pl
from jax.experimental.pallas import tpu as pltpu
from jax.sharding import PartitionSpec as P

CAP = 3
MAIN = 1536
TAIL = 512
WIDTH = MAIN + TAIL
PACK = 8
GROUP = 32
SLAB = PACK * GROUP
SPAN = CAP * GROUP
NT = (((1,), (1,)), ((), ()))
TN = (((0,), (0,)), ((), ()))
ANYWHERE = pl.BlockSpec(memory_space=pl.ANY)
LOCAL = pl.BlockSpec(memory_space=pltpu.VMEM)


def in_hbm(array):
    return pltpu.with_memory_space_constraint(array, pltpu.HBM)


def in_vmem(array):
    return pltpu.with_memory_space_constraint(array, pltpu.VMEM)


def iota(shape, dim):
    return lax.broadcasted_iota(jnp.int32, shape, dim)


def dot(left, right):
    return jnp.dot(left, right, preferred_element_type=jnp.float32)


def column_of(row, count):
    wide = jnp.broadcast_to(row, (count, count))
    return jnp.sum(
        jnp.where(iota((count, count), 0) == iota((count, count), 1), wide, 0.0),
        axis=1,
        keepdims=True,
    )


def ranks(index_row, count, axis):
    expert = column_of(index_row, count)
    same = expert == jnp.broadcast_to(index_row, (count, count))
    first, second = iota((count, count), axis), iota((count, count), 1 - axis)
    found = jnp.sum(jnp.where(same & (first < second), 1.0, 0.0), axis=axis, keepdims=True)
    return found, expert


def slot_code(shape, dim):
    slot = iota(shape, dim)
    group = jnp.zeros_like(slot)
    for edge in range(1, shape[dim] // SPAN):
        group = group + (slot >= SPAN * edge).astype(jnp.int32)
    inner = slot - SPAN * group
    rank = (inner >= GROUP).astype(jnp.int32) + (inner >= 2 * GROUP).astype(jnp.int32)
    return (4 * (GROUP * group + inner - GROUP * rank) + rank).astype(jnp.float32)


def split_matrix():
    out, packed = iota((SLAB, SLAB), 0), iota((SLAB, SLAB), 1)
    match = packed == (out & (GROUP - 1)) * PACK + (out >> 5)
    return jnp.where(match, 1.0, 0.0).astype(jnp.bfloat16)


def join_matrix():
    packed, out = iota((SLAB, SLAB), 0), iota((SLAB, SLAB), 1)
    match = packed == (out & (GROUP - 1)) * PACK + (out >> 5)
    return jnp.where(match, 1.0, 0.0).astype(jnp.bfloat16)


def store_stacked(stacked, value, low, which):
    value = value.astype(jnp.bfloat16)
    width = value.shape[1]
    for group in range(value.shape[0] // SPAN):
        base = SLAB * group
        if low < MAIN:
            stacked[base + SPAN * which : base + SPAN * (which + 1), low : low + width] = value[
                SPAN * group : SPAN * (group + 1)
            ]
        else:
            tail = base + 2 * SPAN + GROUP * which
            for rank in range(CAP):
                start = SPAN * group + GROUP * rank
                column = TAIL * rank + low - MAIN
                stacked[tail : tail + GROUP, column : column + width] = value[
                    start : start + GROUP
                ]


def pack(out, stacked):
    matrix = join_matrix()
    for group in range(out.shape[0] // SLAB):
        part = slice(SLAB * group, SLAB * (group + 1))
        for low in range(0, MAIN, TAIL):
            block = slice(low, low + TAIL)
            out[part, block] = dot(matrix, stacked[part, block]).astype(jnp.bfloat16)


def unpack(packed, matrix, first, second, group):
    base = SPAN * group
    for rank in range(CAP):
        block = slice(TAIL * rank, TAIL * (rank + 1))
        part = dot(matrix, packed[SLAB * group : SLAB * (group + 1), block]).astype(jnp.bfloat16)
        first[base : base + SPAN, block] = part[0:SPAN]
        second[base : base + SPAN, block] = part[SPAN : 2 * SPAN]
        low = base + GROUP * rank
        first[low : low + GROUP, MAIN:] = part[2 * SPAN : 2 * SPAN + GROUP]
        second[low : low + GROUP, MAIN:] = part[2 * SPAN + GROUP :]


def dispatch_kernel(
    index_hbm, weight_hbm, rows_hbm, cot_hbm, out, index, weight, rows, cot, stacked, in_sem
):
    count = rows.shape[0]
    slots = out.shape[0] // PACK * CAP
    loads = [
        pltpu.make_async_copy(source, target, in_sem.at[number])
        for number, (source, target) in enumerate(
            ((index_hbm, index), (weight_hbm, weight), (rows_hbm, rows), (cot_hbm, cot))
        )
    ]
    for load in loads:
        load.start()
    loads[0].wait()
    index_row = index[...].astype(jnp.float32)
    rank_row, _ = ranks(index_row, count, 0)
    place = jnp.where(slot_code((slots, 1), 0) == 4.0 * index_row + rank_row, 1.0, 0.0).astype(
        jnp.bfloat16
    )
    loads[1].wait()
    scale = column_of(weight[...], count)
    loads[2].wait()
    blocks = [slice(0, MAIN), slice(MAIN, WIDTH)]
    for block in blocks:
        store_stacked(stacked, dot(place, rows[:, block]), block.start, 0)
    loads[3].wait()
    for block in blocks:
        grad = (scale * cot[:, block].astype(jnp.float32)).astype(jnp.bfloat16)
        store_stacked(stacked, dot(place, grad), block.start, 1)
    pack(out, stacked)


def dispatch(index, weight, rows, cot, devices):
    count = rows.shape[0]
    return pl.pallas_call(
        dispatch_kernel,
        in_specs=[ANYWHERE] * 4,
        out_specs=LOCAL,
        out_shape=pltpu.VMEM((devices * PACK, MAIN), jnp.bfloat16),
        scratch_shapes=[
            pltpu.VMEM((1, count), jnp.int32),
            pltpu.VMEM((1, count), jnp.float32),
            pltpu.VMEM((count, WIDTH), jnp.bfloat16),
            pltpu.VMEM((count, WIDTH), jnp.bfloat16),
            pltpu.VMEM((devices * PACK, MAIN), jnp.bfloat16),
            pltpu.SemaphoreType.DMA((4,)),
        ],
        compiler_params=pltpu.CompilerParams(vmem_limit_bytes=24 << 20),
        name="dispatch",
    )(in_hbm(index), in_hbm(weight), in_hbm(rows), in_hbm(cot))


def saver(semaphores):
    saves = []

    def save(source, target):
        copy = pltpu.make_async_copy(source, target, semaphores.at[len(saves)])
        copy.start()
        saves.append(copy)

    return save, saves


def expert_kernel(
    got,
    w_gate,
    w_up,
    w_down,
    send_hbm,
    rows_hbm,
    grad_hbm,
    hidden_hbm,
    gate_hbm,
    up_hbm,
    send,
    rows,
    grad,
    hidden,
    gate_pre,
    up_pre,
    stacked,
    out_sem,
):
    save, saves = saver(out_sem)
    groups = got.shape[0] // SLAB
    matrix, join = split_matrix(), join_matrix()
    for group in range(groups):
        unpack(got, matrix, rows, grad, group)
    save(rows, rows_hbm)
    save(grad, grad_hbm)

    gate_act = dot(rows[...], w_gate[...])
    up_act = dot(rows[...], w_up[...])
    hidden_grad = lax.dot_general(
        grad[...], w_down[...], NT, preferred_element_type=jnp.float32
    )
    sigma = jax.nn.sigmoid(gate_act)
    silu_gate = gate_act * sigma
    hidden[...] = (silu_gate * up_act).astype(jnp.bfloat16)
    gate_pre[...] = (
        hidden_grad * up_act * sigma * (1.0 + gate_act * (1.0 - sigma))
    ).astype(jnp.bfloat16)
    up_pre[...] = (hidden_grad * silu_gate).astype(jnp.bfloat16)
    save(hidden, hidden_hbm)
    save(gate_pre, gate_hbm)
    save(up_pre, up_hbm)

    def project(low):
        block = slice(low, low + TAIL)
        store_stacked(stacked, dot(hidden[...], w_down[:, block]), low, 0)
        value = lax.dot_general(
            gate_pre[...], w_gate[block, :], NT, preferred_element_type=jnp.float32
        ) + lax.dot_general(
            up_pre[...], w_up[block, :], NT, preferred_element_type=jnp.float32
        )
        store_stacked(stacked, value, low, 1)

    project(MAIN)
    for rank in range(CAP):
        project(TAIL * rank)
        block = slice(TAIL * rank, TAIL * (rank + 1))
        for group in range(groups):
            part = slice(SLAB * group, SLAB * (group + 1))
            send[part, block] = dot(join, stacked[part, block]).astype(jnp.bfloat16)
        pieces = 1 if rank < CAP - 1 else 2
        for piece in range(pieces):
            part = pl.ds(send.shape[0] // pieces * piece, send.shape[0] // pieces)
            save(send.at[part, block], send_hbm.at[part, block])
    for copy in saves:
        copy.wait()


def expert(got, w_gate, w_up, w_down):
    slots = got.shape[0] // PACK * CAP
    units = w_gate.shape[1]
    shapes = [got.shape] + [(slots, WIDTH)] * 2 + [(slots, units)] * 3
    return pl.pallas_call(
        expert_kernel,
        in_specs=[LOCAL] * 4,
        out_specs=[ANYWHERE] * 6,
        out_shape=[pltpu.HBM(shape, jnp.bfloat16) for shape in shapes],
        scratch_shapes=[pltpu.VMEM(shape, jnp.bfloat16) for shape in shapes]
        + [
            pltpu.VMEM(got.shape, jnp.bfloat16),
            pltpu.SemaphoreType.DMA((6 + CAP,)),
        ],
        compiler_params=pltpu.CompilerParams(vmem_limit_bytes=40 << 20),
        cost_estimate=pl.CostEstimate(
            flops=12 * slots * WIDTH * units,
            bytes_accessed=4 * got.size + 6 * WIDTH * units + 4 * slots * WIDTH,
            transcendentals=slots * units,
        ),
        name="expert",
    )(in_vmem(got), in_vmem(w_gate), in_vmem(w_up), in_vmem(w_down))


def gradient_kernel(
    index,
    weight,
    rows,
    grad,
    hidden,
    gate_pre,
    up_pre,
    gate_hbm,
    up_hbm,
    down_hbm,
    pick,
    scale,
    gate_grad,
    up_grad,
    down_grad,
    out_sem,
):
    count = index.shape[1]
    slots = rows.shape[0]
    save, saves = saver(out_sem)

    for left, right, result, target in (
        (rows, gate_pre, gate_grad, gate_hbm),
        (rows, up_pre, up_grad, up_hbm),
        (hidden, grad, down_grad, down_hbm),
    ):
        for low in range(0, left.shape[1], 256):
            block = slice(low, low + 256)
            result[block, :] = lax.dot_general(
                left[:, block], right[...], TN, preferred_element_type=jnp.float32
            ).astype(jnp.bfloat16)
        save(result, target)
    rank, expert_column = ranks(index[...].astype(jnp.float32), count, 1)
    code = 4.0 * expert_column + rank
    pick[...] = jnp.where(code == slot_code((1, slots), 1), 1.0, 0.0).astype(jnp.bfloat16)
    scale[...] = jnp.broadcast_to(column_of(weight[...], count), scale.shape)
    for copy in saves:
        copy.wait()


def gradients(index, weight, rows, grad, hidden, gate_pre, up_pre):
    count = index.shape[1]
    slots, units = hidden.shape
    tall = (WIDTH, units)
    flat = (units, WIDTH)
    return pl.pallas_call(
        gradient_kernel,
        in_specs=[LOCAL] * 7,
        out_specs=[ANYWHERE] * 3 + [LOCAL] * 2,
        out_shape=[
            pltpu.HBM(tall, jnp.bfloat16),
            pltpu.HBM(tall, jnp.bfloat16),
            pltpu.HBM(flat, jnp.bfloat16),
            pltpu.VMEM((count, slots), jnp.bfloat16),
            pltpu.VMEM((count, 128), jnp.float32),
        ],
        scratch_shapes=[
            pltpu.VMEM(tall, jnp.bfloat16),
            pltpu.VMEM(tall, jnp.bfloat16),
            pltpu.VMEM(flat, jnp.bfloat16),
            pltpu.SemaphoreType.DMA((3,)),
        ],
        compiler_params=pltpu.CompilerParams(vmem_limit_bytes=40 << 20),
        cost_estimate=pl.CostEstimate(
            flops=6 * slots * WIDTH * units,
            bytes_accessed=6 * WIDTH * units + 4 * slots * WIDTH,
            transcendentals=0,
        ),
        name="gradients",
    )(
        in_hbm(index),
        in_hbm(weight),
        in_hbm(rows),
        in_hbm(grad),
        in_hbm(hidden),
        in_hbm(gate_pre),
        in_hbm(up_pre),
    )


def combine_kernel(
    pick,
    scale,
    cot_hbm,
    got,
    out_hbm,
    row_hbm,
    wgrad_hbm,
    cot,
    first,
    second,
    out,
    row,
    wgrad,
    in_sem,
    out_sem,
):
    count = cot.shape[0]
    load = pltpu.make_async_copy(cot_hbm, cot, in_sem)
    load.start()
    matrix = split_matrix()
    for group in range(got.shape[0] // SLAB):
        unpack(got, matrix, first, second, group)
    save, saves = saver(out_sem)
    factor = scale[:, 0:1]
    total = jnp.zeros((count, 1), jnp.float32)

    def store_rows(block):
        row[:, block] = dot(pick[...], second[:, block]).astype(jnp.bfloat16)
        save(row.at[:, block], row_hbm.at[:, block])

    blocks = [slice(low, low + TAIL) for low in range(0, WIDTH, TAIL)]
    for block in blocks:
        if block != blocks[-1]:
            store_rows(block)
        value = dot(pick[...], first[:, block])
        out[:, block] = (factor * value).astype(jnp.bfloat16)
        save(out.at[:, block], out_hbm.at[:, block])
        if block == blocks[0]:
            load.wait()
        total += jnp.sum(cot[:, block].astype(jnp.float32) * value, axis=1, keepdims=True)
    eye = iota((count, count), 0) == iota((count, count), 1)
    wgrad[...] = jnp.sum(jnp.where(eye, total, 0.0), axis=0, keepdims=True)
    save(wgrad, wgrad_hbm)
    store_rows(blocks[-1])
    for copy in saves:
        copy.wait()


def combine(pick, scale, cot, got):
    count = cot.shape[0]
    slots = got.shape[0] // PACK * CAP
    return pl.pallas_call(
        combine_kernel,
        in_specs=[LOCAL, LOCAL, ANYWHERE, LOCAL],
        out_specs=[ANYWHERE] * 3,
        out_shape=[
            pltpu.HBM((count, WIDTH), jnp.bfloat16),
            pltpu.HBM((count, WIDTH), jnp.bfloat16),
            pltpu.HBM((1, count), jnp.float32),
        ],
        scratch_shapes=[
            pltpu.VMEM((count, WIDTH), jnp.bfloat16),
            pltpu.VMEM((slots, WIDTH), jnp.bfloat16),
            pltpu.VMEM((slots, WIDTH), jnp.bfloat16),
            pltpu.VMEM((count, WIDTH), jnp.bfloat16),
            pltpu.VMEM((count, WIDTH), jnp.bfloat16),
            pltpu.VMEM((1, count), jnp.float32),
            pltpu.SemaphoreType.DMA,
            pltpu.SemaphoreType.DMA((2 * WIDTH // TAIL + 1,)),
        ],
        compiler_params=pltpu.CompilerParams(vmem_limit_bytes=24 << 20),
        name="combine",
    )(in_vmem(pick), in_vmem(scale), in_hbm(cot), in_vmem(got))


def exchange(packed, devices):
    moved = lax.all_to_all(
        packed.reshape(devices, PACK, MAIN), "expert", split_axis=0, concat_axis=0, tiled=True
    )
    return moved.reshape(packed.shape)


def local(routed_rows, expert_index, route_weight, cotangent, gate_weight, up_weight, down_weight):
    devices = lax.axis_size("expert")
    count = routed_rows.shape[0]
    index = expert_index.reshape(1, count)
    weight = route_weight.reshape(1, count)
    packed = dispatch(index, weight, routed_rows, cotangent, devices)
    got = exchange(packed, devices)
    send, *saved = expert(got, gate_weight[0], up_weight[0], down_weight[0])
    back = exchange(send, devices)
    gate_grad, up_grad, down_grad, pick, scale = gradients(index, weight, *saved)
    layer_out, row_grad, weight_grad = combine(pick, scale, cotangent, back)
    return (
        layer_out,
        row_grad,
        weight_grad.reshape(count),
        gate_grad[None],
        up_grad[None],
        down_grad[None],
    )


def solution(mesh):
    rows = P("expert", None)
    weights = P("expert", None, None)
    return jax.shard_map(
        local,
        mesh=mesh,
        in_specs=(rows, rows, P("expert"), rows, weights, weights, weights),
        out_specs=(rows, rows, P("expert"), weights, weights, weights),
        check_vma=False,
    )
```

```python
import jax
import jax.numpy as jnp
from jax import lax
from jax.experimental import pallas as pl
from jax.experimental.pallas import tpu as pltpu
from jax.sharding import PartitionSpec as P

CAP = 3
MAIN = 1536
TAIL = 512
WIDTH = MAIN + TAIL
PACK = 8
GROUP = 32
SLAB = PACK * GROUP
SPAN = CAP * GROUP
NT = (((1,), (1,)), ((), ()))
TN = (((0,), (0,)), ((), ()))
ANYWHERE = pl.BlockSpec(memory_space=pl.ANY)
LOCAL = pl.BlockSpec(memory_space=pltpu.VMEM)


def in_hbm(array):
    return pltpu.with_memory_space_constraint(array, pltpu.HBM)


def in_vmem(array):
    return pltpu.with_memory_space_constraint(array, pltpu.VMEM)


def iota(shape, dim):
    return lax.broadcasted_iota(jnp.int32, shape, dim)


def dot(left, right):
    return jnp.dot(left, right, preferred_element_type=jnp.float32)


def column_of(row, count):
    wide = jnp.broadcast_to(row, (count, count))
    return jnp.sum(
        jnp.where(iota((count, count), 0) == iota((count, count), 1), wide, 0.0),
        axis=1,
        keepdims=True,
    )


def ranks(index_row, count, axis):
    expert = column_of(index_row, count)
    same = expert == jnp.broadcast_to(index_row, (count, count))
    first, second = iota((count, count), axis), iota((count, count), 1 - axis)
    found = jnp.sum(jnp.where(same & (first < second), 1.0, 0.0), axis=axis, keepdims=True)
    return found, expert


def slot_code(shape, dim):
    slot = iota(shape, dim)
    group = jnp.zeros_like(slot)
    for edge in range(1, shape[dim] // SPAN):
        group = group + (slot >= SPAN * edge).astype(jnp.int32)
    inner = slot - SPAN * group
    rank = (inner >= GROUP).astype(jnp.int32) + (inner >= 2 * GROUP).astype(jnp.int32)
    return (4 * (GROUP * group + inner - GROUP * rank) + rank).astype(jnp.float32)


def split_matrix():
    out, packed = iota((SLAB, SLAB), 0), iota((SLAB, SLAB), 1)
    match = packed == (out & (GROUP - 1)) * PACK + (out >> 5)
    return jnp.where(match, 1.0, 0.0).astype(jnp.bfloat16)


def join_matrix():
    packed, out = iota((SLAB, SLAB), 0), iota((SLAB, SLAB), 1)
    match = packed == (out & (GROUP - 1)) * PACK + (out >> 5)
    return jnp.where(match, 1.0, 0.0).astype(jnp.bfloat16)


def store_stacked(stacked, value, low, which):
    value = value.astype(jnp.bfloat16)
    width = value.shape[1]
    for group in range(value.shape[0] // SPAN):
        base = SLAB * group
        if low < MAIN:
            stacked[base + SPAN * which : base + SPAN * (which + 1), low : low + width] = value[
                SPAN * group : SPAN * (group + 1)
            ]
        else:
            tail = base + 2 * SPAN + GROUP * which
            for rank in range(CAP):
                start = SPAN * group + GROUP * rank
                column = TAIL * rank + low - MAIN
                stacked[tail : tail + GROUP, column : column + width] = value[
                    start : start + GROUP
                ]


def pack(out, stacked):
    matrix = join_matrix()
    for group in range(out.shape[0] // SLAB):
        part = slice(SLAB * group, SLAB * (group + 1))
        for low in range(0, MAIN, TAIL):
            block = slice(low, low + TAIL)
            out[part, block] = dot(matrix, stacked[part, block]).astype(jnp.bfloat16)


def unpack(packed, matrix, first, second, group):
    base = SPAN * group
    for rank in range(CAP):
        block = slice(TAIL * rank, TAIL * (rank + 1))
        part = dot(matrix, packed[SLAB * group : SLAB * (group + 1), block]).astype(jnp.bfloat16)
        first[base : base + SPAN, block] = part[0:SPAN]
        second[base : base + SPAN, block] = part[SPAN : 2 * SPAN]
        low = base + GROUP * rank
        first[low : low + GROUP, MAIN:] = part[2 * SPAN : 2 * SPAN + GROUP]
        second[low : low + GROUP, MAIN:] = part[2 * SPAN + GROUP :]


def dispatch_kernel(
    index_hbm, weight_hbm, rows_hbm, cot_hbm, out, index, weight, rows, cot, stacked, in_sem
):
    count = rows.shape[0]
    slots = out.shape[0] // PACK * CAP
    loads = [
        pltpu.make_async_copy(source, target, in_sem.at[number])
        for number, (source, target) in enumerate(
            ((index_hbm, index), (weight_hbm, weight), (rows_hbm, rows), (cot_hbm, cot))
        )
    ]
    for load in loads:
        load.start()
    loads[0].wait()
    index_row = index[...].astype(jnp.float32)
    rank_row, _ = ranks(index_row, count, 0)
    place = jnp.where(slot_code((slots, 1), 0) == 4.0 * index_row + rank_row, 1.0, 0.0).astype(
        jnp.bfloat16
    )
    loads[1].wait()
    scale = column_of(weight[...], count)
    loads[2].wait()
    blocks = [slice(0, MAIN), slice(MAIN, WIDTH)]
    for block in blocks:
        store_stacked(stacked, dot(place, rows[:, block]), block.start, 0)
    loads[3].wait()
    for block in blocks:
        grad = (scale * cot[:, block].astype(jnp.float32)).astype(jnp.bfloat16)
        store_stacked(stacked, dot(place, grad), block.start, 1)
    pack(out, stacked)


def dispatch(index, weight, rows, cot, devices):
    count = rows.shape[0]
    return pl.pallas_call(
        dispatch_kernel,
        in_specs=[ANYWHERE] * 4,
        out_specs=LOCAL,
        out_shape=pltpu.VMEM((devices * PACK, MAIN), jnp.bfloat16),
        scratch_shapes=[
            pltpu.VMEM((1, count), jnp.int32),
            pltpu.VMEM((1, count), jnp.float32),
            pltpu.VMEM((count, WIDTH), jnp.bfloat16),
            pltpu.VMEM((count, WIDTH), jnp.bfloat16),
            pltpu.VMEM((devices * PACK, MAIN), jnp.bfloat16),
            pltpu.SemaphoreType.DMA((4,)),
        ],
        compiler_params=pltpu.CompilerParams(vmem_limit_bytes=24 << 20),
        name="dispatch",
    )(in_hbm(index), in_hbm(weight), in_hbm(rows), in_hbm(cot))


def saver(semaphores):
    saves = []

    def save(source, target):
        copy = pltpu.make_async_copy(source, target, semaphores.at[len(saves)])
        copy.start()
        saves.append(copy)

    return save, saves


def expert_kernel(
    got,
    w_gate,
    w_up,
    w_down,
    send_hbm,
    rows_hbm,
    grad_hbm,
    hidden_hbm,
    gate_hbm,
    up_hbm,
    send,
    rows,
    grad,
    hidden,
    gate_pre,
    up_pre,
    stacked,
    out_sem,
):
    save, saves = saver(out_sem)
    groups = got.shape[0] // SLAB
    matrix, join = split_matrix(), join_matrix()
    for group in range(groups):
        unpack(got, matrix, rows, grad, group)
    save(rows, rows_hbm)
    save(grad, grad_hbm)

    gate_act = dot(rows[...], w_gate[...])
    up_act = dot(rows[...], w_up[...])
    hidden_grad = lax.dot_general(
        grad[...], w_down[...], NT, preferred_element_type=jnp.float32
    )
    sigma = jax.nn.sigmoid(gate_act)
    silu_gate = gate_act * sigma
    hidden[...] = (silu_gate * up_act).astype(jnp.bfloat16)
    gate_pre[...] = (
        hidden_grad * up_act * (sigma + silu_gate * (1.0 - sigma))
    ).astype(jnp.bfloat16)
    up_pre[...] = (hidden_grad * silu_gate).astype(jnp.bfloat16)
    save(hidden, hidden_hbm)
    save(gate_pre, gate_hbm)
    save(up_pre, up_hbm)

    def project(low):
        block = slice(low, low + TAIL)
        store_stacked(stacked, dot(hidden[...], w_down[:, block]), low, 0)
        value = lax.dot_general(
            gate_pre[...], w_gate[block, :], NT, preferred_element_type=jnp.float32
        ) + lax.dot_general(
            up_pre[...], w_up[block, :], NT, preferred_element_type=jnp.float32
        )
        store_stacked(stacked, value, low, 1)

    project(MAIN)
    for rank in range(CAP):
        project(TAIL * rank)
        block = slice(TAIL * rank, TAIL * (rank + 1))
        for group in range(groups):
            part = slice(SLAB * group, SLAB * (group + 1))
            send[part, block] = dot(join, stacked[part, block]).astype(jnp.bfloat16)
        pieces = 1 if rank < CAP - 1 else 2
        for piece in range(pieces):
            part = pl.ds(send.shape[0] // pieces * piece, send.shape[0] // pieces)
            save(send.at[part, block], send_hbm.at[part, block])
    for copy in saves:
        copy.wait()


def expert(got, w_gate, w_up, w_down):
    slots = got.shape[0] // PACK * CAP
    units = w_gate.shape[1]
    shapes = [got.shape] + [(slots, WIDTH)] * 2 + [(slots, units)] * 3
    return pl.pallas_call(
        expert_kernel,
        in_specs=[LOCAL] * 4,
        out_specs=[ANYWHERE] * 6,
        out_shape=[pltpu.HBM(shape, jnp.bfloat16) for shape in shapes],
        scratch_shapes=[pltpu.VMEM(shape, jnp.bfloat16) for shape in shapes]
        + [
            pltpu.VMEM(got.shape, jnp.bfloat16),
            pltpu.SemaphoreType.DMA((6 + CAP,)),
        ],
        compiler_params=pltpu.CompilerParams(vmem_limit_bytes=40 << 20),
        cost_estimate=pl.CostEstimate(
            flops=12 * slots * WIDTH * units,
            bytes_accessed=4 * got.size + 6 * WIDTH * units + 4 * slots * WIDTH,
            transcendentals=slots * units,
        ),
        name="expert",
    )(in_vmem(got), in_vmem(w_gate), in_vmem(w_up), in_vmem(w_down))


def gradient_kernel(
    index,
    weight,
    rows,
    grad,
    hidden,
    gate_pre,
    up_pre,
    gate_hbm,
    up_hbm,
    down_hbm,
    pick,
    scale,
    gate_grad,
    up_grad,
    down_grad,
    out_sem,
):
    count = index.shape[1]
    slots = rows.shape[0]
    save, saves = saver(out_sem)

    for left, right, result, target in (
        (rows, gate_pre, gate_grad, gate_hbm),
        (rows, up_pre, up_grad, up_hbm),
        (hidden, grad, down_grad, down_hbm),
    ):
        for low in range(0, left.shape[1], 256):
            block = slice(low, low + 256)
            result[block, :] = lax.dot_general(
                left[:, block], right[...], TN, preferred_element_type=jnp.float32
            ).astype(jnp.bfloat16)
        save(result, target)
    rank, expert_column = ranks(index[...].astype(jnp.float32), count, 1)
    code = 4.0 * expert_column + rank
    pick[...] = jnp.where(code == slot_code((1, slots), 1), 1.0, 0.0).astype(jnp.bfloat16)
    scale[...] = jnp.broadcast_to(column_of(weight[...], count), scale.shape)
    for copy in saves:
        copy.wait()


def gradients(index, weight, rows, grad, hidden, gate_pre, up_pre):
    count = index.shape[1]
    slots, units = hidden.shape
    tall = (WIDTH, units)
    flat = (units, WIDTH)
    return pl.pallas_call(
        gradient_kernel,
        in_specs=[LOCAL] * 7,
        out_specs=[ANYWHERE] * 3 + [LOCAL] * 2,
        out_shape=[
            pltpu.HBM(tall, jnp.bfloat16),
            pltpu.HBM(tall, jnp.bfloat16),
            pltpu.HBM(flat, jnp.bfloat16),
            pltpu.VMEM((count, slots), jnp.bfloat16),
            pltpu.VMEM((count, 128), jnp.float32),
        ],
        scratch_shapes=[
            pltpu.VMEM(tall, jnp.bfloat16),
            pltpu.VMEM(tall, jnp.bfloat16),
            pltpu.VMEM(flat, jnp.bfloat16),
            pltpu.SemaphoreType.DMA((3,)),
        ],
        compiler_params=pltpu.CompilerParams(vmem_limit_bytes=40 << 20),
        cost_estimate=pl.CostEstimate(
            flops=6 * slots * WIDTH * units,
            bytes_accessed=6 * WIDTH * units + 4 * slots * WIDTH,
            transcendentals=0,
        ),
        name="gradients",
    )(
        in_hbm(index),
        in_hbm(weight),
        in_hbm(rows),
        in_hbm(grad),
        in_hbm(hidden),
        in_hbm(gate_pre),
        in_hbm(up_pre),
    )


def combine_kernel(
    pick,
    scale,
    cot_hbm,
    got,
    out_hbm,
    row_hbm,
    wgrad_hbm,
    cot,
    first,
    second,
    out,
    row,
    wgrad,
    in_sem,
    out_sem,
):
    count = cot.shape[0]
    load = pltpu.make_async_copy(cot_hbm, cot, in_sem)
    load.start()
    matrix = split_matrix()
    for group in range(got.shape[0] // SLAB):
        unpack(got, matrix, first, second, group)
    save, saves = saver(out_sem)
    factor = scale[:, 0:1]
    total = jnp.zeros((count, 1), jnp.float32)

    def store_rows(block):
        row[:, block] = dot(pick[...], second[:, block]).astype(jnp.bfloat16)
        save(row.at[:, block], row_hbm.at[:, block])

    blocks = [slice(low, low + TAIL) for low in range(0, WIDTH, TAIL)]
    for block in blocks:
        if block != blocks[-1]:
            store_rows(block)
        value = dot(pick[...], first[:, block])
        out[:, block] = (factor * value).astype(jnp.bfloat16)
        save(out.at[:, block], out_hbm.at[:, block])
        if block == blocks[0]:
            load.wait()
        total += jnp.sum(cot[:, block].astype(jnp.float32) * value, axis=1, keepdims=True)
    eye = iota((count, count), 0) == iota((count, count), 1)
    wgrad[...] = jnp.sum(jnp.where(eye, total, 0.0), axis=0, keepdims=True)
    save(wgrad, wgrad_hbm)
    store_rows(blocks[-1])
    for copy in saves:
        copy.wait()


def combine(pick, scale, cot, got):
    count = cot.shape[0]
    slots = got.shape[0] // PACK * CAP
    return pl.pallas_call(
        combine_kernel,
        in_specs=[LOCAL, LOCAL, ANYWHERE, LOCAL],
        out_specs=[ANYWHERE] * 3,
        out_shape=[
            pltpu.HBM((count, WIDTH), jnp.bfloat16),
            pltpu.HBM((count, WIDTH), jnp.bfloat16),
            pltpu.HBM((1, count), jnp.float32),
        ],
        scratch_shapes=[
            pltpu.VMEM((count, WIDTH), jnp.bfloat16),
            pltpu.VMEM((slots, WIDTH), jnp.bfloat16),
            pltpu.VMEM((slots, WIDTH), jnp.bfloat16),
            pltpu.VMEM((count, WIDTH), jnp.bfloat16),
            pltpu.VMEM((count, WIDTH), jnp.bfloat16),
            pltpu.VMEM((1, count), jnp.float32),
            pltpu.SemaphoreType.DMA,
            pltpu.SemaphoreType.DMA((2 * WIDTH // TAIL + 1,)),
        ],
        compiler_params=pltpu.CompilerParams(vmem_limit_bytes=24 << 20),
        name="combine",
    )(in_vmem(pick), in_vmem(scale), in_hbm(cot), in_vmem(got))


def exchange(packed, devices):
    moved = lax.all_to_all(
        packed.reshape(devices, PACK, MAIN), "expert", split_axis=0, concat_axis=0, tiled=True
    )
    return moved.reshape(packed.shape)


def local(routed_rows, expert_index, route_weight, cotangent, gate_weight, up_weight, down_weight):
    devices = lax.axis_size("expert")
    count = routed_rows.shape[0]
    index = expert_index.reshape(1, count)
    weight = route_weight.reshape(1, count)
    packed = dispatch(index, weight, routed_rows, cotangent, devices)
    got = exchange(packed, devices)
    send, *saved = expert(got, gate_weight[0], up_weight[0], down_weight[0])
    back = exchange(send, devices)
    gate_grad, up_grad, down_grad, pick, scale = gradients(index, weight, *saved)
    layer_out, row_grad, weight_grad = combine(pick, scale, cotangent, back)
    return (
        layer_out,
        row_grad,
        weight_grad.reshape(count),
        gate_grad[None],
        up_grad[None],
        down_grad[None],
    )


def solution(mesh):
    rows = P("expert", None)
    weights = P("expert", None, None)
    return jax.shard_map(
        local,
        mesh=mesh,
        in_specs=(rows, rows, P("expert"), rows, weights, weights, weights),
        out_specs=(rows, rows, P("expert"), weights, weights, weights),
        check_vma=False,
    )
```
